32 devices in a mesh: groups: 2 (over y), seq: 4 (over z), head: 4 (over x, core).
Axes of the slice: x: 2, y: 2, z: 4, core: 2. Of those that a mesh axis runs over, the one named last changes fastest.
Arguments:
- queries: bfloat16 [8, 2, 64, 128], P(('groups', 'seq'), None, 'head'), parts along dimension 0, may hold values from -128 to 128
- new_keys: bfloat16 [8, 2, 8, 128], P(('groups', 'seq'), None, 'head'), parts along dimension 0, may hold values from -24 to 24
- new_values: bfloat16 [8, 2, 8, 128], P(('groups', 'seq'), None, 'head'), parts along dimension 0, may hold values from -6 to 6
- shared_keys: bfloat16 [2048, 8, 128], P(('groups', 'seq'), 'head'), parts along dimension 0, may hold values from -4 to 4
- shared_values: bfloat16 [2048, 8, 128], P(('groups', 'seq'), 'head'), parts along dimension 0, may hold values from -6 to 6
- fewshot_keys: bfloat16 [4096, 8, 128], P(('groups', 'seq'), 'head'), parts along dimension 0, may hold values from -9 to 9
- fewshot_values: bfloat16 [4096, 8, 128], P(('groups', 'seq'), 'head'), parts along dimension 0, may hold values from -6 to 6
- suffix_keys: bfloat16 [16, 128, 8, 128], P(('groups', 'seq'), None, 'head'), parts along dimension 0, may hold values from -12 to 12
- suffix_values: bfloat16 [16, 128, 8, 128], P(('groups', 'seq'), None, 'head'), parts along dimension 0, may hold values from -6 to 6
- request_prefix: int32 [8], P('groups'), parts along dimension 0, may hold values from 0 to 3, as said below
- prefix_owner: int32 [8], P('groups'), parts along dimension 0, may hold values from 0 to 3, each once
- prefix_length: int32 [8], P('groups'), parts along dimension 0, may hold values from 128 to 512, as said below
- suffix_slot: int32 [8], P('groups'), parts along dimension 0, may hold values from 0 to 7, as said below
- suffix_length: int32 [8], P('groups'), parts along dimension 0, may hold values from 1 to 128, as said below
Outputs:
- attn: bfloat16 [8, 2, 64, 128], P(('groups', 'seq'), None, 'head'), parts along dimension 0
The draws below stay inside these ranges and needn't reach their ends.
There are 2 independent parts, one for each index of `groups`. The reference program is written for one: setup_inputs(seed, part) draws one part's arguments, and reference() takes and returns one part's arrays. A program takes and returns all parts, laid end to end along the dimension named above; each array names one. Nothing has to cross between parts.
Inputs may be any that keep to these rules, and one draw needn't show every extreme that they name: `request_prefix`: no prefix is used by more than 2 requests; some prefix by exactly 2. `prefix_length`: the longest prefix has exactly 512 positions. `suffix_slot`: distinct for distinct requests; slot s lies on index s // 2 of seq; some index of seq holds exactly 2 requests' suffixes. `suffix_length`: the longest suffix has exactly 128 positions.
All inputs are finite; a program needn't handle non-finite values.
Results may differ from the reference program's by a relative error of at most 0.004.
Values may be sent and summed in bfloat16 or wider, within the bound.
A program may use at most 64 MiB of HBM per device.

```python
import jax
import jax.numpy as jnp
from jax import lax

HEADS = 64
KV_HEADS = 8
HEAD_DIM = 128
STEPS = 2
FS_MAX = 512
SUF_MAX = 128
REQUESTS = 4
SHARED = 1024
PREFIXES = 4
FS_CAP = 2
SUF_CAP = 2
SLOTS = 8


def base_queries(key):
    return jax.random.truncated_normal(jax.random.fold_in(key, 101), -4.0, 4.0, (REQUESTS, STEPS, HEADS, HEAD_DIM), jnp.float32) * 2.0


def shared_law(key):
    return jax.random.truncated_normal(jax.random.fold_in(key, 202), -4.0, 4.0, (SHARED, KV_HEADS, HEAD_DIM), jnp.float32)


def draw_shared_keys(key, part):
    return shared_law(key).astype(jnp.bfloat16)


def draw_queries(key, part):
    query_all = base_queries(key)
    return query_all.astype(jnp.bfloat16)


def draw_new_keys(key, part):
    query_all = base_queries(key).reshape(REQUESTS, STEPS, KV_HEADS, HEADS // KV_HEADS, HEAD_DIM)
    average = jnp.mean(query_all, axis=3)
    noise = jax.random.truncated_normal(jax.random.fold_in(key, 404), -4.0, 4.0, (REQUESTS, STEPS, KV_HEADS, HEAD_DIM), jnp.float32)
    return (2.0 * average + noise).astype(jnp.bfloat16)


def draw_request_prefix(key, part):
    key_rank, key_noise, key_order = jax.random.split(jax.random.fold_in(key, 505), 3)
    ranking = jax.random.permutation(key_rank, PREFIXES)
    slot_prefix = jnp.arange(PREFIXES * FS_CAP, dtype=jnp.int32) // FS_CAP
    slot_rank = ranking[slot_prefix]
    noise = jax.random.randint(key_noise, (PREFIXES * FS_CAP,), 0, 4096)
    popular = slot_rank < max(PREFIXES // 4, 1)
    priority = jnp.where(slot_rank == 0, 1 << 24, jnp.where(popular, noise * 4, noise))
    chosen = jnp.argsort(-priority, stable=True)[:REQUESTS]
    shuffle = jax.random.permutation(key_order, REQUESTS)
    return (chosen[shuffle] // FS_CAP).astype(jnp.int32)


def draw_suffix_slot(key, part):
    key_full, key_noise, key_order = jax.random.split(jax.random.fold_in(key, 606), 3)
    full_dev = jax.random.randint(key_full, (), 0, SLOTS // SUF_CAP)
    noise = jax.random.randint(key_noise, (SLOTS,), 0, 1 << 20)
    priority = jnp.where(jnp.arange(SLOTS, dtype=jnp.int32) // SUF_CAP == full_dev, 1 << 24, noise)
    chosen = jnp.argsort(-priority, stable=True)[:REQUESTS]
    shuffle = jax.random.permutation(key_order, REQUESTS)
    return chosen[shuffle].astype(jnp.int32)


def draw_prefix_length(key, part):
    key_len, key_top = jax.random.split(jax.random.fold_in(key, 707), 2)
    lengths = jax.random.randint(key_len, (PREFIXES,), FS_MAX // 4, FS_MAX + 1)
    longest = jax.random.randint(key_top, (), 0, PREFIXES)
    return lengths.at[longest].set(FS_MAX).astype(jnp.int32)


def draw_suffix_length(key, part):
    key_len, key_top = jax.random.split(jax.random.fold_in(key, 808), 2)
    lengths = jax.random.randint(key_len, (REQUESTS,), 1, SUF_MAX + 1)
    longest = jax.random.randint(key_top, (), 0, REQUESTS)
    return lengths.at[longest].set(SUF_MAX).astype(jnp.int32)


def shard_levels(rng, extent, cuts, smallest, largest):
    def one(dim, shards_of):
        steps = jax.random.uniform(jax.random.fold_in(jax.random.fold_in(rng, 6), dim), (shards_of,), jnp.float32, smallest / len(cuts), largest / len(cuts))
        return jnp.repeat(jnp.exp(steps), extent[dim] // shards_of).reshape((-1,) + (1,) * (len(extent) - dim - 1))

    level = one(*cuts[0])
    for cut in cuts[1:]:
        level = level * one(*cut)
    return level


def centred(key, extent, width, bound, shards=(), kind=jnp.bfloat16):
    gain = shard_levels(key, extent, shards, -0.22, 0.18) if shards else 1.0
    values = jax.random.normal(key, extent, jnp.float32) * width * gain
    return jnp.minimum(jnp.maximum(values, -bound), bound).astype(kind)


def setup_inputs(seed: int = 0, part: int = 0) -> dict:
    seeds = jax.random.split(jax.random.key(seed), 15)
    part_keys = jax.random.split(jax.random.fold_in(seeds[14], part), 15)
    return {
        "queries": draw_queries(jax.random.fold_in(jax.random.fold_in(seeds[14], part), 71), part),
        "new_keys": draw_new_keys(jax.random.fold_in(jax.random.fold_in(seeds[14], part), 71), part),
        "new_values": centred(part_keys[2], (REQUESTS, STEPS, KV_HEADS, HEAD_DIM), 1.0, 6.0, ((0, 4), (2, 4))),
        "shared_keys": draw_shared_keys(jax.random.fold_in(jax.random.fold_in(seeds[14], part), 71), part),
        "shared_values": centred(part_keys[4], (SHARED, KV_HEADS, HEAD_DIM), 1.0, 6.0, ((0, 4), (1, 4))),
        "fewshot_keys": centred(part_keys[5], (PREFIXES * FS_MAX, KV_HEADS, HEAD_DIM), 1.5, 9.0, ((0, 4), (1, 4))),
        "fewshot_values": centred(part_keys[6], (PREFIXES * FS_MAX, KV_HEADS, HEAD_DIM), 1.0, 6.0, ((0, 4), (1, 4))),
        "suffix_keys": centred(part_keys[7], (SLOTS, SUF_MAX, KV_HEADS, HEAD_DIM), 2.0, 12.0, ((0, 4), (2, 4))),
        "suffix_values": centred(part_keys[8], (SLOTS, SUF_MAX, KV_HEADS, HEAD_DIM), 1.0, 6.0, ((0, 4), (2, 4))),
        "request_prefix": draw_request_prefix(jax.random.fold_in(jax.random.fold_in(seeds[14], part), 71), part),
        "prefix_owner": jax.random.permutation(part_keys[10], PREFIXES).astype(jnp.int32),
        "prefix_length": draw_prefix_length(jax.random.fold_in(jax.random.fold_in(seeds[14], part), 71), part),
        "suffix_slot": draw_suffix_slot(jax.random.fold_in(jax.random.fold_in(seeds[14], part), 71), part),
        "suffix_length": draw_suffix_length(jax.random.fold_in(jax.random.fold_in(seeds[14], part), 71), part),
    }


very_low = -1.0e30


def scores_of(query_rows, keys_level, inv_root):
    return jnp.einsum("tgqd,lgd->tgql", query_rows, keys_level, precision=lax.Precision.HIGHEST) * inv_root


def values_of(weights, values_level):
    rounded = lax.optimization_barrier(weights.astype(jnp.bfloat16)).astype(jnp.float32)
    return jnp.einsum("tgql,lgd->tgqd", rounded, values_level, precision=lax.Precision.HIGHEST)


def reference(queries, new_keys, new_values, shared_keys, shared_values, fewshot_keys, fewshot_values, suffix_keys, suffix_values, request_prefix, prefix_owner, prefix_length, suffix_slot, suffix_length):
    group_size = HEADS // KV_HEADS
    inv_root = HEAD_DIM ** -0.5
    keys_shared = shared_keys.astype(jnp.float32)
    values_shared = shared_values.astype(jnp.float32)
    step_pos = jnp.arange(STEPS)
    causal = (step_pos[:, None] >= step_pos[None, :])[:, None, None, :]

    def one_request(request):
        query_rows = queries[request].astype(jnp.float32).reshape(STEPS, KV_HEADS, group_size, HEAD_DIM)
        chosen = request_prefix[request]
        owner_slot = prefix_owner[chosen]
        few_len = prefix_length[chosen]
        first_row = (owner_slot * FS_MAX).astype(jnp.int32)
        keys_few = lax.dynamic_slice_in_dim(fewshot_keys, first_row, FS_MAX, 0).astype(jnp.float32)
        values_few = lax.dynamic_slice_in_dim(fewshot_values, first_row, FS_MAX, 0).astype(jnp.float32)
        suffix_index = suffix_slot[request].astype(jnp.int32)
        keys_suffix = lax.dynamic_index_in_dim(suffix_keys, suffix_index, 0, keepdims=False).astype(jnp.float32)
        values_suffix = lax.dynamic_index_in_dim(suffix_values, suffix_index, 0, keepdims=False).astype(jnp.float32)
        suf_len = suffix_length[request]
        keys_new = new_keys[request].astype(jnp.float32)
        values_new = new_values[request].astype(jnp.float32)
        level_masks = [
            (jnp.arange(SHARED) >= 0)[None, None, None, :],
            (jnp.arange(FS_MAX) < few_len)[None, None, None, :],
            (jnp.arange(SUF_MAX) < suf_len)[None, None, None, :],
            causal,
        ]
        level_keys = [keys_shared, keys_few, keys_suffix, keys_new]
        level_values = [values_shared, values_few, values_suffix, values_new]
        level_scores = [jnp.where(mask_level, scores_of(query_rows, keys_level, inv_root), very_low) for mask_level, keys_level in zip(level_masks, level_keys)]
        row_top = jnp.max(jnp.stack([jnp.max(level, axis=-1) for level in level_scores]), axis=0)
        level_weights = [jnp.where(mask_level, jnp.exp(level - row_top[..., None]), 0.0) for mask_level, level in zip(level_masks, level_scores)]
        totals = sum(jnp.sum(level, axis=-1) for level in level_weights)
        numer = sum(values_of(level, values_level) for level, values_level in zip(level_weights, level_values))
        return (numer / totals[..., None]).reshape(STEPS, HEADS, HEAD_DIM).astype(jnp.bfloat16)

    return lax.map(one_request, jnp.arange(REQUESTS, dtype=jnp.int32))
```

```python
import functools

import jax
import jax.numpy as jnp
from jax import lax
from jax.experimental import pallas as pl
from jax.experimental.pallas import tpu as pltpu
from jax.sharding import PartitionSpec as P

very_low = -1e30


def each(count, step, carry):
    if count <= 8:
        for index in range(count):
            carry = step(index, carry)
        return carry
    return lax.fori_loop(0, count, step, carry)


def attend_kernel(
    sizes,
    q_hbm,
    nk_hbm,
    nv_hbm,
    sk_hbm,
    sv_hbm,
    fk_hbm,
    fv_hbm,
    uk_hbm,
    uv_hbm,
    prefix_hbm,
    owner_hbm,
    plen_hbm,
    slot_hbm,
    slen_hbm,
    out_ref,
    q_own,
    nk_own,
    nv_own,
    k_raw,
    v_raw,
    k_cat,
    v_cat,
    prefix_s,
    owner_s,
    plen_s,
    slot_s,
    slen_s,
    q_got,
    sum_out,
    sum_got,
    stat_out,
    stat_got,
    local_sem,
    q_send,
    q_recv,
    sum_send,
    sum_recv,
    stat_send,
    stat_recv,
):
    n, kv, steps, group, width, shared_len, few_len, slots, suf_len = sizes
    me = lax.axis_index("seq")
    heads = kv * group
    rows = steps * heads
    tiles = rows // 8
    keys = shared_len + few_len + slots * suf_len
    inv_root = width ** (-0.5)

    def peer(distance):
        return lax.rem(me + distance, n)

    barrier = pltpu.get_barrier_semaphore()

    def greet(index, carry):
        pl.semaphore_signal(barrier, inc=1, device_id={"seq": peer(index + 1)})
        return carry

    each(n - 1, greet, 0)

    locals_ = []

    def bring(source, target):
        copy = pltpu.make_async_copy(source, target, local_sem.at[len(locals_)])
        copy.start()
        locals_.append(copy)

    bring(q_hbm, q_own)
    first, second, last = (
        shared_len * kv,
        (shared_len + few_len) * kv,
        keys * kv,
    )
    bring(sk_hbm, k_raw.at[pl.ds(0, first)])
    bring(fk_hbm, k_raw.at[pl.ds(first, second - first)])
    bring(uk_hbm, k_raw.at[pl.ds(second, last - second)])
    bring(sv_hbm, v_raw.at[pl.ds(0, first)])
    bring(fv_hbm, v_raw.at[pl.ds(first, second - first)])
    bring(uv_hbm, v_raw.at[pl.ds(second, last - second)])
    bring(prefix_hbm, prefix_s)
    bring(owner_hbm, owner_s)
    bring(plen_hbm, plen_s)
    bring(slot_hbm, slot_s)
    bring(slen_hbm, slen_s)
    bring(nk_hbm, nk_own)
    bring(nv_hbm, nv_own)

    locals_[0].wait()
    pl.semaphore_wait(barrier, n - 1)

    def query_copy(distance):
        return pltpu.make_async_remote_copy(
            src_ref=q_own,
            dst_ref=q_got.at[distance],
            send_sem=q_send.at[distance],
            recv_sem=q_recv.at[distance],
            device_id={"seq": peer(distance)},
            device_id_type=pl.DeviceIdType.MESH,
        )

    def sum_copy(distance):
        return pltpu.make_async_remote_copy(
            src_ref=sum_out.at[distance],
            dst_ref=sum_got.at[distance],
            send_sem=sum_send.at[distance],
            recv_sem=sum_recv.at[distance],
            device_id={"seq": peer(distance)},
            device_id_type=pl.DeviceIdType.MESH,
        )

    def stat_copy(distance):
        return pltpu.make_async_remote_copy(
            src_ref=stat_out.at[distance],
            dst_ref=stat_got.at[distance],
            send_sem=stat_send.at[distance],
            recv_sem=stat_recv.at[distance],
            device_id={"seq": peer(distance)},
            device_id_type=pl.DeviceIdType.MESH,
        )

    order = (2, 1, 3) if n == 4 else None

    def away(index, near_first):
        if order is None:
            return index + 1
        return (order[1:] + order[:1])[index] if near_first else order[index]

    def send_query(index, carry):
        query_copy(away(index, False)).start()
        return carry

    each(n - 1, send_query, 0)

    block = 256 // kv
    row_id = lax.broadcasted_iota(jnp.int32, (256, 256), 0)
    col_id = lax.broadcasted_iota(jnp.int32, (256, 256), 1)
    source_row = lax.rem(row_id, block) * kv + row_id // block
    sorter = jnp.where(col_id == source_row, 1.0, 0.0).astype(jnp.bfloat16)

    def sort_rows(raw, cat):
        for b in range(keys // block):
            part = jnp.dot(
                sorter, raw[pl.ds(b * 256, 256), :], preferred_element_type=jnp.float32
            ).astype(jnp.bfloat16)
            for h in range(kv):
                cat[pl.ds(b * block, block), pl.ds(h * width, width)] = part[
                    h * block : (h + 1) * block
                ]

    for index in (1, 2, 3):
        locals_[index].wait()
    sort_rows(k_raw, k_cat)
    for index in (4, 5, 6):
        locals_[index].wait()
    sort_rows(v_raw, v_cat)
    for index in range(7, 14):
        locals_[index].wait()

    head_of_row = lax.rem(lax.broadcasted_iota(jnp.int32, (rows, width), 0), heads) // group
    picks = [jnp.where(head_of_row == h, 1.0, 0.0).astype(jnp.bfloat16) for h in range(kv)]
    column = lax.broadcasted_iota(jnp.int32, (1, keys), 1)

    def partial_sums(query, request):
        home = owner_s[prefix_s[request]]
        few = jnp.where(home == me, plen_s[prefix_s[request]], 0)
        limit = jnp.where(column < shared_len, keys, shared_len + few)
        for s in range(slots):
            start = shared_len + few_len + s * suf_len
            length = jnp.where(slot_s[request] == me * slots + s, slen_s[request], 0)
            limit = jnp.where(column >= start, start + length, limit)
        bias = jnp.where(column < limit, 0.0, very_low)
        wide = jnp.concatenate([query * pick for pick in picks], axis=1)
        scores = (
            lax.dot_general(
                wide,
                k_cat[...],
                (((1,), (1,)), ((), ())),
                preferred_element_type=jnp.float32,
            )
            * inv_root
            + bias
        )
        top = jnp.max(scores, axis=1, keepdims=True)
        weights = jnp.exp(scores - top)
        total = jnp.sum(weights, axis=1, keepdims=True)
        both = jnp.dot(
            weights.astype(jnp.bfloat16), v_cat[...], preferred_element_type=jnp.float32
        )
        numer = both[:, :width]
        for h in range(1, kv):
            numer = jnp.where(head_of_row == h, both[:, h * width : (h + 1) * width], numer)
        return top, total, numer

    lane = lax.broadcasted_iota(jnp.int32, (8, 128), 1)

    def pack_stats(top, total):
        packed = jnp.zeros((8, 128), jnp.float32)
        for tile in range(tiles):
            part = slice(tile * 8, tile * 8 + 8)
            packed = jnp.where(lane == tile, top[part], packed)
            packed = jnp.where(lane == tile + tiles, total[part], packed)
        return packed

    own_query = q_own[...]
    own_top, own_total, own_numer = partial_sums(own_query, me)
    fresh = steps * kv
    new_scores = (
        lax.dot_general(
            own_query,
            nk_own[...],
            (((1,), (1,)), ((), ())),
            preferred_element_type=jnp.float32,
        )
        * inv_root
    )
    new_row = lax.broadcasted_iota(jnp.int32, (rows, fresh), 0)
    new_col = lax.broadcasted_iota(jnp.int32, (rows, fresh), 1)
    seen = (lax.rem(new_row, heads) // group == lax.rem(new_col, kv)) & (
        new_col // kv <= new_row // heads
    )
    new_scores = jnp.where(seen, new_scores, very_low)
    joint_top = jnp.maximum(own_top, jnp.max(new_scores, axis=1, keepdims=True))
    old_factor = jnp.exp(own_top - joint_top)
    new_weights = jnp.exp(new_scores - joint_top)
    own_total = own_total * old_factor + jnp.sum(new_weights, axis=1, keepdims=True)
    own_numer = own_numer * old_factor
    rounded = new_weights.astype(jnp.bfloat16).astype(jnp.float32)
    new_values = nv_own[...].astype(jnp.float32)
    for j in range(fresh):
        own_numer = own_numer + rounded[:, j : j + 1] * new_values[j : j + 1, :]
    own_stat = pack_stats(joint_top, own_total)

    def serve(index, carry):
        distance = away(index, True)
        query_copy(distance).wait_recv()
        top, total, numer = partial_sums(q_got[distance], lax.rem(me + n - distance, n))
        back = n - distance
        sum_out[back] = numer.astype(jnp.bfloat16)
        sum_copy(back).start()
        stat_out[back] = pack_stats(top, total)
        stat_copy(back).start()
        return carry

    each(n - 1, serve, 0)

    def find_top(index, highest):
        stat_copy(index + 1).wait_recv()
        return jnp.maximum(highest, stat_got[index + 1])

    highest = each(n - 1, find_top, own_stat)

    def add_total(index, total):
        stat = stat_got[index + 1]
        return total + pltpu.roll(jnp.exp(stat - highest), tiles, 1) * stat

    own_scale = jnp.exp(own_stat - highest)
    total = each(n - 1, add_total, pltpu.roll(own_scale, tiles, 1) * own_stat)
    inverse = 1.0 / jnp.where(lane < tiles, pltpu.roll(total, 128 - tiles, 1), 1.0)

    def spread_rows(scale):
        return jnp.concatenate(
            [jnp.broadcast_to(scale[:, t : t + 1], (8, width)) for t in range(tiles)], axis=0
        )

    def add_sum(index, result):
        sum_copy(index + 1).wait_recv()
        scale = jnp.exp(stat_got[index + 1] - highest) * inverse
        return result + sum_got[index + 1].astype(jnp.float32) * spread_rows(scale)

    result = each(n - 1, add_sum, own_numer * spread_rows(own_scale * inverse))
    out_ref[...] = result.astype(jnp.bfloat16)

    def settle(index, carry):
        query_copy(index + 1).wait_send()
        sum_copy(index + 1).wait_send()
        stat_copy(index + 1).wait_send()
        return carry

    each(n - 1, settle, 0)


def per_device(
    queries,
    new_keys,
    new_values,
    shared_keys,
    shared_values,
    fewshot_keys,
    fewshot_values,
    suffix_keys,
    suffix_values,
    *lists,
):
    n = lax.axis_size("seq")
    steps, heads, width = queries.shape[1:]
    kv = new_keys.shape[2]
    group = heads // kv
    rows = steps * heads
    shared_len, few_len = shared_keys.shape[0], fewshot_keys.shape[0]
    slots, suf_len = suffix_keys.shape[:2]
    keys = shared_len + few_len + slots * suf_len
    sizes = (n, kv, steps, group, width, shared_len, few_len, slots, suf_len)
    flat = [
        item.reshape(-1, width)
        for item in (
            queries,
            new_keys,
            new_values,
            shared_keys,
            shared_values,
            fewshot_keys,
            fewshot_values,
            suffix_keys,
            suffix_values,
        )
    ]
    half, full = jnp.bfloat16, jnp.float32
    dma = pltpu.SemaphoreType.DMA
    result = pl.pallas_call(
        functools.partial(attend_kernel, sizes),
        out_shape=jax.ShapeDtypeStruct((rows, width), half),
        in_specs=[pl.BlockSpec(memory_space=pltpu.HBM)] * 14,
        out_specs=pl.BlockSpec(memory_space=pltpu.VMEM),
        scratch_shapes=[
            pltpu.VMEM((rows, width), half),
            pltpu.VMEM((steps * kv, width), half),
            pltpu.VMEM((steps * kv, width), half),
            pltpu.VMEM((keys * kv, width), half),
            pltpu.VMEM((keys * kv, width), half),
            pltpu.VMEM((keys, kv * width), half),
            pltpu.VMEM((keys, kv * width), half),
        ]
        + [pltpu.SMEM(item.shape, jnp.int32) for item in lists]
        + [
            pltpu.VMEM((n, rows, width), half),
            pltpu.VMEM((n, rows, width), half),
            pltpu.VMEM((n, rows, width), half),
            pltpu.VMEM((n, 8, 128), full),
            pltpu.VMEM((n, 8, 128), full),
            dma((14,)),
        ]
        + [dma((n,))] * 6,
        compiler_params=pltpu.CompilerParams(collective_id=0, has_side_effects=True),
        name="prefix_attend",
    )(*flat, *lists)
    return result.reshape(queries.shape)


def solution(mesh):
    seq_rows = P(("groups", "seq"), None, "head", None)
    seq_keys = P(("groups", "seq"), "head", None)
    return jax.shard_map(
        per_device,
        mesh=mesh,
        in_specs=(seq_rows,) * 3 + (seq_keys,) * 4 + (seq_rows,) * 2 + (P("groups"),) * 5,
        out_specs=seq_rows,
        check_vma=False,
    )
```

```python
import functools

import jax
import jax.numpy as jnp
from jax import lax
from jax.experimental import pallas as pl
from jax.experimental.pallas import tpu as pltpu
from jax.sharding import PartitionSpec as P

very_low = -1e30


def each(count, step, carry):
    if count <= 8:
        for index in range(count):
            carry = step(index, carry)
        return carry
    return lax.fori_loop(0, count, step, carry)


def attend_kernel(
    sizes,
    q_hbm,
    nk_hbm,
    nv_hbm,
    sk_hbm,
    sv_hbm,
    fk_hbm,
    fv_hbm,
    uk_hbm,
    uv_hbm,
    prefix_hbm,
    owner_hbm,
    plen_hbm,
    slot_hbm,
    slen_hbm,
    out_ref,
    nk_own,
    nv_own,
    k_raw,
    v_raw,
    k_cat,
    v_cat,
    prefix_s,
    owner_s,
    plen_s,
    slot_s,
    slen_s,
    q_got,
    sum_out,
    sum_got,
    stat_out,
    stat_got,
    bias_rows,
    local_sem,
    q_send,
    q_recv,
    sum_send,
    sum_recv,
    stat_send,
    stat_recv,
):
    n, kv, steps, group, width, shared_len, few_len, slots, suf_len = sizes
    me = lax.axis_index("seq")
    heads = kv * group
    rows = steps * heads
    tiles = rows // 8
    keys = shared_len + few_len + slots * suf_len
    inv_root = width ** (-0.5)

    def peer(distance):
        return lax.rem(me + distance, n)

    barrier = pltpu.get_barrier_semaphore()

    def greet(index, carry):
        pl.semaphore_signal(barrier, inc=1, device_id={"seq": peer(index + 1)})
        return carry

    each(n - 1, greet, 0)

    locals_ = []

    def bring(source, target):
        copy = pltpu.make_async_copy(source, target, local_sem.at[len(locals_)])
        copy.start()
        locals_.append(copy)

    bring(q_hbm, q_got.at[0])
    first, second, last = (
        shared_len * kv,
        (shared_len + few_len) * kv,
        keys * kv,
    )
    bring(sk_hbm, k_raw.at[pl.ds(0, first)])
    bring(fk_hbm, k_raw.at[pl.ds(first, second - first)])
    bring(uk_hbm, k_raw.at[pl.ds(second, last - second)])
    bring(sv_hbm, v_raw.at[pl.ds(0, first)])
    bring(fv_hbm, v_raw.at[pl.ds(first, second - first)])
    bring(uv_hbm, v_raw.at[pl.ds(second, last - second)])
    bring(prefix_hbm, prefix_s)
    bring(owner_hbm, owner_s)
    bring(plen_hbm, plen_s)
    bring(slot_hbm, slot_s)
    bring(slen_hbm, slen_s)
    bring(nk_hbm, nk_own)
    bring(nv_hbm, nv_own)

    locals_[0].wait()
    pl.semaphore_wait(barrier, n - 1)

    def query_copy(distance):
        return pltpu.make_async_remote_copy(
            src_ref=q_got.at[0],
            dst_ref=q_got.at[distance],
            send_sem=q_send.at[distance],
            recv_sem=q_recv.at[distance],
            device_id={"seq": peer(distance)},
            device_id_type=pl.DeviceIdType.MESH,
        )

    def sum_copy(distance):
        return pltpu.make_async_remote_copy(
            src_ref=sum_out.at[distance],
            dst_ref=sum_got.at[distance],
            send_sem=sum_send.at[distance],
            recv_sem=sum_recv.at[distance],
            device_id={"seq": peer(distance)},
            device_id_type=pl.DeviceIdType.MESH,
        )

    def stat_copy(distance):
        return pltpu.make_async_remote_copy(
            src_ref=stat_out.at[distance],
            dst_ref=stat_got.at[distance],
            send_sem=stat_send.at[distance],
            recv_sem=stat_recv.at[distance],
            device_id={"seq": peer(distance)},
            device_id_type=pl.DeviceIdType.MESH,
        )

    def send_query(index, carry):
        query_copy(index + 1).start()
        return carry

    each(n - 1, send_query, 0)

    block = 256 // kv
    row_id = lax.broadcasted_iota(jnp.int32, (256, 256), 0)
    col_id = lax.broadcasted_iota(jnp.int32, (256, 256), 1)
    source_row = lax.rem(row_id, block) * kv + row_id // block
    sorter = jnp.where(col_id == source_row, 1.0, 0.0).astype(jnp.bfloat16)

    def sort_rows(raw, cat):
        for b in range(keys // block):
            part = jnp.dot(
                sorter, raw[pl.ds(b * 256, 256), :], preferred_element_type=jnp.float32
            ).astype(jnp.bfloat16)
            for h in range(kv):
                cat[pl.ds(b * block, block), pl.ds(h * width, width)] = part[
                    h * block : (h + 1) * block
                ]

    for index in range(7, 14):
        locals_[index].wait()
    column = lax.broadcasted_iota(jnp.int32, (1, keys), 1)

    def mask_row(request, carry):
        home = owner_s[prefix_s[request]]
        few = jnp.where(home == me, plen_s[prefix_s[request]], 0)
        limit = jnp.where(column < shared_len, keys, shared_len + few)
        for s in range(slots):
            start = shared_len + few_len + s * suf_len
            length = jnp.where(slot_s[request] == me * slots + s, slen_s[request], 0)
            limit = jnp.where(column >= start, start + length, limit)
        bias_rows[pl.ds(request, 1), :] = jnp.where(column < limit, 0.0, very_low)
        return carry

    each(n, mask_row, 0)

    for index in (1, 2, 3):
        locals_[index].wait()
    sort_rows(k_raw, k_cat)
    for index in (4, 5, 6):
        locals_[index].wait()
    sort_rows(v_raw, v_cat)

    head_of_row = lax.rem(lax.broadcasted_iota(jnp.int32, (rows, width), 0), heads) // group
    picks = [jnp.where(head_of_row == h, 1.0, 0.0).astype(jnp.bfloat16) for h in range(kv)]
    lane = lax.broadcasted_iota(jnp.int32, (8, 128), 1)

    def pack_stats(top, total):
        packed = jnp.zeros((8, 128), jnp.float32)
        for tile in range(tiles):
            part = slice(tile * 8, tile * 8 + 8)
            packed = jnp.where(lane == tile, top[part], packed)
            packed = jnp.where(lane == tile + tiles, total[part], packed)
        return packed

    own_query = q_got[0]
    fresh = steps * kv
    new_scores = (
        lax.dot_general(
            own_query,
            nk_own[...],
            (((1,), (1,)), ((), ())),
            preferred_element_type=jnp.float32,
        )
        * inv_root
    )
    new_row = lax.broadcasted_iota(jnp.int32, (rows, fresh), 0)
    new_col = lax.broadcasted_iota(jnp.int32, (rows, fresh), 1)
    seen = (lax.rem(new_row, heads) // group == lax.rem(new_col, kv)) & (
        new_col // kv <= new_row // heads
    )
    new_scores = jnp.where(seen, new_scores, very_low)
    new_top = jnp.max(new_scores, axis=1, keepdims=True)
    new_weights = jnp.exp(new_scores - new_top)
    rounded = new_weights.astype(jnp.bfloat16).astype(jnp.float32)
    new_values = nv_own[...].astype(jnp.float32)
    new_numer = jnp.zeros((rows, width), jnp.float32)
    for j in range(fresh):
        new_numer = new_numer + rounded[:, j : j + 1] * new_values[j : j + 1, :]
    new_stat = pack_stats(new_top, jnp.sum(new_weights, axis=1, keepdims=True))

    def distance_from(request):
        return lax.rem(me + n - request, n)

    def serve(request, carry):
        distance = distance_from(request)
        back = lax.rem(request + n - me, n)
        remote = distance != 0

        @pl.when(remote)
        def _():
            query_copy(distance).wait_recv()

        wide = jnp.concatenate([q_got[distance] * pick for pick in picks], axis=1)
        scores = (
            lax.dot_general(
                wide,
                k_cat[...],
                (((1,), (1,)), ((), ())),
                preferred_element_type=jnp.float32,
            )
            * inv_root
            + bias_rows[pl.ds(request, 1), :]
        )
        top = jnp.max(scores, axis=1, keepdims=True)
        weights = jnp.exp(scores - top)
        total = jnp.sum(weights, axis=1, keepdims=True)
        stat_out[back] = pack_stats(top, total)

        @pl.when(remote)
        def _():
            stat_copy(back).start()

        both = jnp.dot(
            weights.astype(jnp.bfloat16), v_cat[...], preferred_element_type=jnp.float32
        )
        numer = both[:, :width]
        for h in range(1, kv):
            numer = jnp.where(head_of_row == h, both[:, h * width : (h + 1) * width], numer)
        sum_out[back] = numer.astype(jnp.bfloat16)

        @pl.when(remote)
        def _():
            sum_copy(back).start()

        return carry

    each(n, serve, 0)

    def source_of(index):
        return distance_from(index + jnp.where(index >= me, 1, 0))

    own_stat = stat_out[0]

    def find_top(index, highest):
        slot = source_of(index)
        stat_copy(slot).wait_recv()
        return jnp.maximum(highest, stat_got[slot])

    highest = each(n - 1, find_top, jnp.maximum(own_stat, new_stat))

    def share(stat):
        return pltpu.roll(jnp.exp(stat - highest), tiles, 1) * stat

    def add_total(index, total):
        return total + share(stat_got[source_of(index)])

    total = each(n - 1, add_total, share(own_stat) + share(new_stat))
    inverse = 1.0 / jnp.where(lane < tiles, pltpu.roll(total, 128 - tiles, 1), 1.0)

    def spread_rows(stat):
        scale = jnp.exp(stat - highest) * inverse
        return jnp.concatenate(
            [jnp.broadcast_to(scale[:, t : t + 1], (8, width)) for t in range(tiles)], axis=0
        )

    def add_sum(index, result):
        slot = source_of(index)
        scale = spread_rows(stat_got[slot])
        sum_copy(slot).wait_recv()
        return result + sum_got[slot].astype(jnp.float32) * scale

    start = new_numer * spread_rows(new_stat) + sum_out[0].astype(jnp.float32) * spread_rows(
        own_stat
    )
    out_ref[...] = each(n - 1, add_sum, start).astype(jnp.bfloat16)

    def settle(index, carry):
        query_copy(index + 1).wait_send()
        sum_copy(index + 1).wait_send()
        stat_copy(index + 1).wait_send()
        return carry

    each(n - 1, settle, 0)


def per_device(
    queries,
    new_keys,
    new_values,
    shared_keys,
    shared_values,
    fewshot_keys,
    fewshot_values,
    suffix_keys,
    suffix_values,
    *lists,
):
    n = lax.axis_size("seq")
    steps, heads, width = queries.shape[1:]
    kv = new_keys.shape[2]
    group = heads // kv
    rows = steps * heads
    shared_len, few_len = shared_keys.shape[0], fewshot_keys.shape[0]
    slots, suf_len = suffix_keys.shape[:2]
    keys = shared_len + few_len + slots * suf_len
    sizes = (n, kv, steps, group, width, shared_len, few_len, slots, suf_len)
    flat = [
        item.reshape(-1, width)
        for item in (
            queries,
            new_keys,
            new_values,
            shared_keys,
            shared_values,
            fewshot_keys,
            fewshot_values,
            suffix_keys,
            suffix_values,
        )
    ]
    half, full = jnp.bfloat16, jnp.float32
    dma = pltpu.SemaphoreType.DMA
    result = pl.pallas_call(
        functools.partial(attend_kernel, sizes),
        out_shape=pltpu.VMEM((rows, width), half),
        in_specs=[pl.BlockSpec(memory_space=pltpu.HBM)] * 14,
        out_specs=pl.BlockSpec(memory_space=pltpu.VMEM),
        scratch_shapes=[
            pltpu.VMEM((steps * kv, width), half),
            pltpu.VMEM((steps * kv, width), half),
            pltpu.VMEM((keys * kv, width), half),
            pltpu.VMEM((keys * kv, width), half),
            pltpu.VMEM((keys, kv * width), half),
            pltpu.VMEM((keys, kv * width), half),
        ]
        + [pltpu.SMEM(item.shape, jnp.int32) for item in lists]
        + [
            pltpu.VMEM((n, rows, width), half),
            pltpu.VMEM((n, rows, width), half),
            pltpu.VMEM((n, rows, width), half),
            pltpu.VMEM((n, 8, 128), full),
            pltpu.VMEM((n, 8, 128), full),
            pltpu.VMEM((n, keys), full),
            dma((14,)),
        ]
        + [dma((n,))] * 6,
        compiler_params=pltpu.CompilerParams(collective_id=0, has_side_effects=True),
        name="prefix_attend",
    )(*flat, *lists)
    return result.reshape(queries.shape)


def solution(mesh):
    seq_rows = P(("groups", "seq"), None, "head", None)
    seq_keys = P(("groups", "seq"), "head", None)
    return jax.shard_map(
        per_device,
        mesh=mesh,
        in_specs=(seq_rows,) * 3 + (seq_keys,) * 4 + (seq_rows,) * 2 + (P("groups"),) * 5,
        out_specs=seq_rows,
        check_vma=False,
    )
```

```python
import functools

import jax
import jax.numpy as jnp
from jax import lax
from jax.experimental import pallas as pl
from jax.experimental.pallas import tpu as pltpu
from jax.sharding import PartitionSpec as P

very_low = -1e30


def each(count, step, carry):
    if count <= 8:
        for index in range(count):
            carry = step(index, carry)
        return carry
    return lax.fori_loop(0, count, step, carry)


def attend_kernel(
    sizes,
    q_hbm,
    nk_hbm,
    nv_hbm,
    sk_hbm,
    sv_hbm,
    fk_hbm,
    fv_hbm,
    uk_hbm,
    uv_hbm,
    prefix_hbm,
    owner_hbm,
    plen_hbm,
    slot_hbm,
    slen_hbm,
    out_ref,
    nk_own,
    nv_own,
    k_raw,
    v_raw,
    k_cat,
    v_cat,
    prefix_s,
    owner_s,
    plen_s,
    slot_s,
    slen_s,
    q_got,
    sum_out,
    sum_got,
    stat_out,
    stat_got,
    bias_rows,
    local_sem,
    q_send,
    q_recv,
    sum_send,
    sum_recv,
    stat_send,
    stat_recv,
):
    n, kv, steps, group, width, shared_len, few_len, slots, suf_len = sizes
    me = lax.axis_index("seq")
    heads = kv * group
    rows = steps * heads
    tiles = rows // 8
    keys = shared_len + few_len + slots * suf_len
    inv_root = width ** (-0.5)

    def peer(distance):
        return lax.rem(me + distance, n)

    barrier = pltpu.get_barrier_semaphore()

    def greet(index, carry):
        pl.semaphore_signal(barrier, inc=1, device_id={"seq": peer(index + 1)})
        return carry

    each(n - 1, greet, 0)

    locals_ = []

    def bring(source, target):
        copy = pltpu.make_async_copy(source, target, local_sem.at[len(locals_)])
        copy.start()
        locals_.append(copy)

    bring(q_hbm, q_got.at[0])
    first, second, last = (
        shared_len * kv,
        (shared_len + few_len) * kv,
        keys * kv,
    )
    bring(sk_hbm, k_raw.at[pl.ds(0, first)])
    bring(fk_hbm, k_raw.at[pl.ds(first, second - first)])
    bring(uk_hbm, k_raw.at[pl.ds(second, last - second)])
    bring(sv_hbm, v_raw.at[pl.ds(0, first)])
    bring(fv_hbm, v_raw.at[pl.ds(first, second - first)])
    bring(uv_hbm, v_raw.at[pl.ds(second, last - second)])
    bring(prefix_hbm, prefix_s)
    bring(owner_hbm, owner_s)
    bring(plen_hbm, plen_s)
    bring(slot_hbm, slot_s)
    bring(slen_hbm, slen_s)
    bring(nk_hbm, nk_own)
    bring(nv_hbm, nv_own)

    locals_[0].wait()
    pl.semaphore_wait(barrier, n - 1)

    def query_copy(distance):
        return pltpu.make_async_remote_copy(
            src_ref=q_got.at[0],
            dst_ref=q_got.at[distance],
            send_sem=q_send.at[0],
            recv_sem=q_recv.at[distance],
            device_id={"seq": peer(distance)},
            device_id_type=pl.DeviceIdType.MESH,
        )

    def sum_copy(distance):
        return pltpu.make_async_remote_copy(
            src_ref=sum_out.at[distance],
            dst_ref=sum_got.at[distance],
            send_sem=sum_send.at[0],
            recv_sem=sum_recv.at[distance],
            device_id={"seq": peer(distance)},
            device_id_type=pl.DeviceIdType.MESH,
        )

    def stat_copy(distance):
        return pltpu.make_async_remote_copy(
            src_ref=stat_out.at[distance],
            dst_ref=stat_got.at[distance],
            send_sem=stat_send.at[0],
            recv_sem=stat_recv.at[distance],
            device_id={"seq": peer(distance)},
            device_id_type=pl.DeviceIdType.MESH,
        )

    def send_query(index, carry):
        query_copy(index + 1).start()
        return carry

    each(n - 1, send_query, 0)

    block = 256 // kv
    row_id = lax.broadcasted_iota(jnp.int32, (256, 256), 0)
    col_id = lax.broadcasted_iota(jnp.int32, (256, 256), 1)
    source_row = lax.rem(row_id, block) * kv + row_id // block
    sorter = jnp.where(col_id == source_row, 1.0, 0.0).astype(jnp.bfloat16)

    def sort_rows(raw, cat):
        for b in range(keys // block):
            part = jnp.dot(
                sorter, raw[pl.ds(b * 256, 256), :], preferred_element_type=jnp.float32
            ).astype(jnp.bfloat16)
            for h in range(kv):
                cat[pl.ds(b * block, block), pl.ds(h * width, width)] = part[
                    h * block : (h + 1) * block
                ]

    for index in range(7, 14):
        locals_[index].wait()
    column = lax.broadcasted_iota(jnp.int32, (1, keys), 1)

    def mask_row(request, carry):
        home = owner_s[prefix_s[request]]
        few = jnp.where(home == me, plen_s[prefix_s[request]], 0)
        limit = jnp.where(column < shared_len, keys, shared_len + few)
        for s in range(slots):
            start = shared_len + few_len + s * suf_len
            length = jnp.where(slot_s[request] == me * slots + s, slen_s[request], 0)
            limit = jnp.where(column >= start, start + length, limit)
        bias_rows[pl.ds(request, 1), :] = jnp.where(column < limit, 0.0, very_low)
        return carry

    each(n, mask_row, 0)

    for index in (1, 2, 3):
        locals_[index].wait()
    sort_rows(k_raw, k_cat)
    for index in (4, 5, 6):
        locals_[index].wait()
    sort_rows(v_raw, v_cat)

    head_of_row = lax.rem(lax.broadcasted_iota(jnp.int32, (rows, width), 0), heads) // group
    picks = [jnp.where(head_of_row == h, 1.0, 0.0).astype(jnp.bfloat16) for h in range(kv)]
    lane = lax.broadcasted_iota(jnp.int32, (8, 128), 1)

    def pack_stats(top, total):
        packed = jnp.zeros((8, 128), jnp.float32)
        for tile in range(tiles):
            part = slice(tile * 8, tile * 8 + 8)
            packed = jnp.where(lane == tile, top[part], packed)
            packed = jnp.where(lane == tile + tiles, total[part], packed)
        return packed

    own_query = q_got[0]
    fresh = steps * kv
    new_scores = (
        lax.dot_general(
            own_query,
            nk_own[...],
            (((1,), (1,)), ((), ())),
            preferred_element_type=jnp.float32,
        )
        * inv_root
    )
    new_row = lax.broadcasted_iota(jnp.int32, (rows, fresh), 0)
    new_col = lax.broadcasted_iota(jnp.int32, (rows, fresh), 1)
    seen = (lax.rem(new_row, heads) // group == lax.rem(new_col, kv)) & (
        new_col // kv <= new_row // heads
    )
    new_scores = jnp.where(seen, new_scores, very_low)
    new_top = jnp.max(new_scores, axis=1, keepdims=True)
    new_weights = jnp.exp(new_scores - new_top)
    rounded = new_weights.astype(jnp.bfloat16).astype(jnp.float32)
    new_values = nv_own[...].astype(jnp.float32)
    new_numer = jnp.zeros((rows, width), jnp.float32)
    for j in range(fresh):
        new_numer = new_numer + rounded[:, j : j + 1] * new_values[j : j + 1, :]
    new_stat = pack_stats(new_top, jnp.sum(new_weights, axis=1, keepdims=True))

    def distance_from(request):
        return lax.rem(me + n - request, n)

    def serve(request, carry):
        distance = distance_from(request)
        back = lax.rem(request + n - me, n)
        remote = distance != 0

        @pl.when(remote)
        def _():
            query_copy(distance).wait_recv()

        wide = jnp.concatenate([q_got[distance] * pick for pick in picks], axis=1)
        scores = (
            lax.dot_general(
                wide,
                k_cat[...],
                (((1,), (1,)), ((), ())),
                preferred_element_type=jnp.float32,
            )
            * inv_root
            + bias_rows[pl.ds(request, 1), :]
        )
        top = jnp.max(scores, axis=1, keepdims=True)
        weights = jnp.exp(scores - top)
        total = jnp.sum(weights, axis=1, keepdims=True)
        stat_out[back] = pack_stats(top, total)

        @pl.when(remote)
        def _():
            stat_copy(back).start()

        both = jnp.dot(
            weights.astype(jnp.bfloat16), v_cat[...], preferred_element_type=jnp.float32
        )
        numer = both[:, :width]
        for h in range(1, kv):
            numer = jnp.where(head_of_row == h, both[:, h * width : (h + 1) * width], numer)
        sum_out[back] = numer.astype(jnp.bfloat16)

        @pl.when(remote)
        def _():
            sum_copy(back).start()

        return carry

    each(n, serve, 0)

    def source_of(index):
        return distance_from(index + jnp.where(index >= me, 1, 0))

    own_stat = stat_out[0]

    def find_top(index, highest):
        slot = source_of(index)
        stat_copy(slot).wait_recv()
        return jnp.maximum(highest, stat_got[slot])

    highest = each(n - 1, find_top, jnp.maximum(own_stat, new_stat))

    def share(stat):
        return pltpu.roll(jnp.exp(stat - highest), tiles, 1) * stat

    def add_total(index, total):
        return total + share(stat_got[source_of(index)])

    total = each(n - 1, add_total, share(own_stat) + share(new_stat))
    inverse = 1.0 / jnp.where(lane < tiles, pltpu.roll(total, 128 - tiles, 1), 1.0)

    def spread_rows(stat):
        scale = jnp.exp(stat - highest) * inverse
        return jnp.concatenate(
            [jnp.broadcast_to(scale[:, t : t + 1], (8, width)) for t in range(tiles)], axis=0
        )

    def add_sum(index, result):
        slot = source_of(index)
        scale = spread_rows(stat_got[slot])
        sum_copy(slot).wait_recv()
        return result + sum_got[slot].astype(jnp.float32) * scale

    start = new_numer * spread_rows(new_stat) + sum_out[0].astype(jnp.float32) * spread_rows(
        own_stat
    )
    out_ref[...] = each(n - 1, add_sum, start).astype(jnp.bfloat16)

    for sent, sem in ((sum_got, q_send), (sum_out, sum_send), (stat_out, stat_send)):
        part = sent.at[pl.ds(1, n - 1)]
        pltpu.make_async_copy(part, part, sem.at[0]).wait()


def per_device(
    queries,
    new_keys,
    new_values,
    shared_keys,
    shared_values,
    fewshot_keys,
    fewshot_values,
    suffix_keys,
    suffix_values,
    *lists,
):
    n = lax.axis_size("seq")
    steps, heads, width = queries.shape[1:]
    kv = new_keys.shape[2]
    group = heads // kv
    rows = steps * heads
    shared_len, few_len = shared_keys.shape[0], fewshot_keys.shape[0]
    slots, suf_len = suffix_keys.shape[:2]
    keys = shared_len + few_len + slots * suf_len
    sizes = (n, kv, steps, group, width, shared_len, few_len, slots, suf_len)
    flat = [
        item.reshape(-1, width)
        for item in (
            queries,
            new_keys,
            new_values,
            shared_keys,
            shared_values,
            fewshot_keys,
            fewshot_values,
            suffix_keys,
            suffix_values,
        )
    ]
    half, full = jnp.bfloat16, jnp.float32
    dma = pltpu.SemaphoreType.DMA
    result = pl.pallas_call(
        functools.partial(attend_kernel, sizes),
        out_shape=pltpu.VMEM((rows, width), half),
        in_specs=[pl.BlockSpec(memory_space=pltpu.HBM)] * 14,
        out_specs=pl.BlockSpec(memory_space=pltpu.VMEM),
        scratch_shapes=[
            pltpu.VMEM((steps * kv, width), half),
            pltpu.VMEM((steps * kv, width), half),
            pltpu.VMEM((keys * kv, width), half),
            pltpu.VMEM((keys * kv, width), half),
            pltpu.VMEM((keys, kv * width), half),
            pltpu.VMEM((keys, kv * width), half),
        ]
        + [pltpu.SMEM(item.shape, jnp.int32) for item in lists]
        + [
            pltpu.VMEM((n, rows, width), half),
            pltpu.VMEM((n, rows, width), half),
            pltpu.VMEM((n, rows, width), half),
            pltpu.VMEM((n, 8, 128), full),
            pltpu.VMEM((n, 8, 128), full),
            pltpu.VMEM((n, keys), full),
            dma((14,)),
        ]
        + [dma((1,)), dma((n,))] * 3,
        compiler_params=pltpu.CompilerParams(collective_id=0, has_side_effects=True),
        name="prefix_attend",
    )(*flat, *lists)
    return result.reshape(queries.shape)


def solution(mesh):
    seq_rows = P(("groups", "seq"), None, "head", None)
    seq_keys = P(("groups", "seq"), "head", None)
    return jax.shard_map(
        per_device,
        mesh=mesh,
        in_specs=(seq_rows,) * 3 + (seq_keys,) * 4 + (seq_rows,) * 2 + (P("groups"),) * 5,
        out_specs=seq_rows,
        check_vma=False,
    )
```
